32 devices in a mesh: grp: 2 (over y), rows: 4 (over z), img: 2 (over x), tp: 2 (over core).
Axes of the slice: x: 2, y: 2, z: 4, core: 2. Of those that a mesh axis runs over, the one named last changes fastest.
Arguments:
- features: bfloat16 [16, 28, 2, 7168], P(('grp', 'img'), 'rows', 'tp'), parts along dimension 0, may hold values from -8 to 8
- gn_gain: float32 [128], P('tp'), may hold values from 0.5 to 1.5
- conv_w: bfloat16 [3, 3, 3, 128], P(None, None, None, 'tp'), may hold values from -0.1875 to 0.1875
- patch_w: bfloat16 [1280, 588], P('rows'), may hold values from -0.25 to 0.25
- pos_emb: bfloat16 [64, 1280], replicated, may hold values from -3 to 3
- ln1_gain: float32 [1280], replicated, may hold values from 0.5 to 1.5
- qkv_w: bfloat16 [1280, 3, 1280], P('rows', None, 'tp'), may hold values from -3 to 3
- out_w: bfloat16 [1280, 1280], P('rows', 'tp'), may hold values from -0.15625 to 0.15625
- final_gain: float32 [1280], replicated, may hold values from 0.5 to 1.5
- head_w: float32 [1280], replicated, may hold values from -0.15625 to 0.15625
- owner_slot: int32 [4, 4], P(('grp', 'img')), parts along dimension 0, may hold values from 0 to 3, each once within a row
Outputs:
- grad_features: bfloat16 [16, 28, 2, 7168], P(('grp', 'img'), 'rows', 'tp'), parts along dimension 0
- slot_reward: float32 [16], P(('grp', 'img', 'rows')), parts along dimension 0
The draws below stay inside these ranges and needn't reach their ends.
There are 2 independent parts, one for each index of `grp`. The reference program is written for one: setup_inputs(seed, part) draws one part's arguments, and reference() takes and returns one part's arrays. A program takes and returns all parts, laid end to end along the dimension named above; an argument that names none is the same for every part. Nothing has to cross between parts.
Inputs may be any that keep to these rules, and one draw needn't show every extreme that they name: Each row is a permutation: image g * 4 + j is scored in slot owner_slot[g, j] of its image group.
All inputs are finite; a program needn't handle non-finite values.
Results may differ from the reference program's by a relative error of at most 0.028.
Values may be sent and summed in bfloat16 or wider, within the bound.
A program may use at most 128 MiB of HBM per device.

```python
import math
import jax
import jax.numpy as jnp
from jax import lax

C = 128
GROUPS = 32
D = 1280
HEADS = 16
PATCH = 14
HALF_C = 64
HEAD_DIM = 80
H = 28
W = 112
TOKENS = 64
PIX = 588
IMG_SLAB = 4
IMAGES = 8
N_IMG = 2


def draw_features(key, part):
    noise_key = jax.random.fold_in(key, 0)
    full_shape = (IMAGES, H, W, C)
    position = jnp.arange(H, dtype=jnp.float32) / (H - 1)
    noise_draw = jax.random.normal(noise_key, full_shape, jnp.float32)
    row_scale = 0.5 + position
    values = noise_draw * row_scale[None, :, None, None]
    values = jnp.clip(values, -8.0, 8.0)
    values = values.reshape(IMAGES, H, W, 2, HALF_C).transpose(0, 1, 3, 2, 4).reshape(IMAGES, H, 2, W * HALF_C)
    return values.astype(jnp.bfloat16)


def draw_qkv_w(key, part):
    base_key = jax.random.fold_in(key, 0)
    weights = jax.random.normal(base_key, (D, 3, HEADS, HEAD_DIM), jnp.float32)
    weights = jnp.clip(weights, -3.0, 3.0) / jnp.sqrt(jnp.float32(D))
    return weights.reshape(D, 3, HEADS * HEAD_DIM).astype(jnp.bfloat16)


def steps_of(key, extent, shards, least, top_value):
    factor_of, own = 1.0, jax.random.fold_in(key, 6)
    for axis_at, blocks in shards:
        steps = jnp.exp(jax.random.uniform(jax.random.fold_in(own, axis_at), (blocks,), jnp.float32, least / len(shards), top_value / len(shards)))
        factor_of = factor_of * jnp.repeat(steps, extent[axis_at] // blocks).reshape([-1 if axis == axis_at else 1 for axis in range(len(extent))])
    return factor_of


def bell_draw(stream_key, dims, scale, bound, pieces=(), held_as=jnp.bfloat16):
    values = scale * jax.random.normal(stream_key, dims, jnp.float32)
    if pieces:
        values = values * steps_of(stream_key, dims, pieces, -0.22, 0.18)
    return jnp.clip(values, -bound, bound).astype(held_as)


def setup_inputs(seed: int = 0, part: int = 0) -> dict:
    key_list = jax.random.split(jax.random.key(seed), 12)
    part_keys = jax.random.split(jax.random.fold_in(key_list[11], part), 12)
    features = draw_features(jax.random.fold_in(jax.random.fold_in(key_list[11], part), 71), part)
    gn_gain = jnp.clip(1.0 + 0.1 * jax.random.normal(key_list[1], (C,), jnp.float32), 0.5, 1.5)
    conv_w = bell_draw(key_list[2], (3, 3, 3, C), (9 * C) ** -0.5, 0.1875, ((3, 2),))
    patch_w = bell_draw(key_list[3], (D, PIX), PIX ** -0.5, 0.25, ((0, 4),))
    pos_emb = bell_draw(key_list[4], (TOKENS, D), 0.5, 3.0)
    ln1_gain = jnp.clip(1.0 + 0.1 * jax.random.normal(key_list[5], (D,), jnp.float32), 0.5, 1.5)
    qkv_w = draw_qkv_w(jax.random.fold_in(key_list[11], 71), part)
    out_w = bell_draw(key_list[7], (D, HEADS * HEAD_DIM), D ** -0.5, 0.15625, ((0, 4), (1, 2)))
    final_gain = jnp.clip(1.0 + 0.1 * jax.random.normal(key_list[8], (D,), jnp.float32), 0.5, 1.5)
    head_w = bell_draw(key_list[9], (D,), D ** -0.5, 0.15625, (), jnp.float32)
    owner_slot = jax.vmap(lambda own: jax.random.permutation(own, IMG_SLAB))(jax.random.split(part_keys[10], N_IMG)).reshape((N_IMG, IMG_SLAB)).astype(jnp.int32)
    return dict(features=features, gn_gain=gn_gain, conv_w=conv_w, patch_w=patch_w, pos_emb=pos_emb, ln1_gain=ln1_gain, qkv_w=qkv_w, out_w=out_w, final_gain=final_gain, head_w=head_w, owner_slot=owner_slot)


EPS_GROUP = 1e-06
EPS_LAYER = 1e-05

def round_half(values):
    return lax.optimization_barrier(values.astype(jnp.bfloat16)).astype(jnp.float32)

def layer_norm(values, scale_vec):
    average = lax.optimization_barrier(jnp.mean(values, axis=-1, keepdims=True))
    centred = values - average
    spread = lax.optimization_barrier(jnp.mean(centred * centred, axis=-1, keepdims=True))
    inverse = lax.rsqrt(spread + EPS_LAYER)
    normed = centred * inverse
    return (normed * scale_vec, normed, inverse)

def layer_norm_back(upstream, normed, inverse, scale_vec):
    scaled = upstream * scale_vec
    mean_one = lax.optimization_barrier(jnp.mean(scaled, axis=-1, keepdims=True))
    mean_two = lax.optimization_barrier(jnp.mean(scaled * normed, axis=-1, keepdims=True))
    return inverse * (scaled - mean_one - normed * mean_two)

def silu_parts(values):
    sigmoid = jax.nn.sigmoid(values)
    return (values * sigmoid, sigmoid * (1.0 + values * (1.0 - sigmoid)))

def group_sums(values, groups_here):
    grouped = values.reshape(values.shape[0], -1, groups_here, values.shape[3] // groups_here)
    return lax.optimization_barrier(jnp.sum(grouped, axis=(1, 3)))

def spread_groups(per_group, chan_count):
    return jnp.repeat(per_group, chan_count // per_group.shape[1], axis=1)[:, None, None, :]

def conv_forward(rim_rows, kernel):
    image_count, rows_rim, col_count, chan_count = rim_rows.shape
    rows_here = rows_rim - 2
    padded = jnp.pad(rim_rows, ((0, 0), (0, 0), (1, 1), (0, 0)))
    accum = jnp.zeros((image_count * rows_here * col_count, 3), jnp.float32)
    for offset_y in range(3):
        for offset_x in range(3):
            window = padded[:, offset_y:offset_y + rows_here, offset_x:offset_x + col_count, :]
            accum = accum + jnp.dot(window.reshape(-1, chan_count), kernel[:, offset_y, offset_x, :].T, preferred_element_type=jnp.float32)
    return accum.reshape(image_count, rows_here, col_count, 3)

def conv_back(grad_rim, kernel):
    image_count, rows_rim, col_count, _ = grad_rim.shape
    rows_here = rows_rim - 2
    padded = jnp.pad(grad_rim, ((0, 0), (0, 0), (1, 1), (0, 0)))
    accum = jnp.zeros((image_count * rows_here * col_count, kernel.shape[3]), jnp.float32)
    for offset_y in range(3):
        for offset_x in range(3):
            window = padded[:, 2 - offset_y:2 - offset_y + rows_here, 2 - offset_x:2 - offset_x + col_count, :]
            accum = accum + jnp.dot(window.reshape(-1, 3), kernel[:, offset_y, offset_x, :], preferred_element_type=jnp.float32)
    return accum.reshape(image_count, rows_here, col_count, kernel.shape[3])

def to_patches(picture):
    larger = jnp.repeat(jnp.repeat(picture, 2, axis=0), 2, axis=1)
    patch_rows = larger.shape[0] // PATCH
    patch_cols = larger.shape[1] // PATCH
    blocks = larger.reshape(patch_rows, PATCH, patch_cols, PATCH, 3).transpose(0, 2, 1, 3, 4)
    return blocks.reshape(patch_rows * patch_cols, PATCH * PATCH * 3)

def from_patches(grads_in, rows_full, col_count):
    patch_rows = rows_full * 2 // PATCH
    patch_cols = col_count * 2 // PATCH
    blocks = grads_in.reshape(patch_rows, patch_cols, PATCH, PATCH, 3).transpose(0, 2, 1, 3, 4)
    larger = blocks.reshape(rows_full, 2, col_count, 2, 3)
    return lax.optimization_barrier(jnp.sum(larger, axis=(1, 3)))

def soft_weights(q_heads, k_heads):
    factor = 1.0 / math.sqrt(HEAD_DIM)
    scores = jnp.einsum('thd,shd->hts', q_heads, k_heads) * factor
    row_max = lax.optimization_barrier(jnp.max(scores, axis=-1, keepdims=True))
    exp_scores = jnp.exp(scores - row_max)
    return exp_scores / lax.optimization_barrier(jnp.sum(exp_scores, axis=-1, keepdims=True))

def split_heads(rows_in):
    return rows_in.reshape(rows_in.shape[0], rows_in.shape[1] // HEAD_DIM, HEAD_DIM).astype(jnp.float32)

def attend(queries, key_rows, value_rows):
    prob_soft = soft_weights(split_heads(queries), split_heads(key_rows))
    attended = jnp.einsum('hts,shd->thd', round_half(prob_soft), split_heads(value_rows))
    return attended.reshape(queries.shape).astype(jnp.bfloat16)

def attend_back(queries, key_rows, value_rows, head_grad):
    factor = 1.0 / math.sqrt(HEAD_DIM)
    q_heads = split_heads(queries)
    k_heads = split_heads(key_rows)
    v_heads = split_heads(value_rows)
    g_heads = split_heads(head_grad)
    prob_soft = soft_weights(q_heads, k_heads)
    dprob = jnp.einsum('thd,shd->hts', g_heads, v_heads)
    dvalue = jnp.einsum('hts,thd->shd', round_half(prob_soft), g_heads).reshape(queries.shape).astype(jnp.bfloat16)
    dscores = prob_soft * (dprob - lax.optimization_barrier(jnp.sum(dprob * prob_soft, axis=-1, keepdims=True))) * factor
    dscores = round_half(dscores)
    dquery = jnp.einsum('hts,shd->thd', dscores, k_heads).reshape(queries.shape).astype(jnp.bfloat16)
    dkey = jnp.einsum('hts,thd->shd', dscores, q_heads).reshape(queries.shape).astype(jnp.bfloat16)
    return (dquery, dkey, dvalue)

def reference(features, gn_gain, conv_w, patch_w, pos_emb, ln1_gain, qkv_w, out_w, final_gain, head_w, owner_slot):
    half_heads = D // 2
    half_chan = C // 2
    qkv_flat = qkv_w.reshape(D, 3, D)
    out_flat = out_w.reshape(D, D)
    count_group = H * W * (C // GROUPS)
    feat_maps = features.reshape(IMAGES, H, 2, W, HALF_C).transpose(0, 1, 3, 2, 4).reshape(IMAGES, H, W, C)

    def one_image(feat_one):
        feat_float = feat_one.astype(jnp.float32)[None]
        totals = group_sums(feat_float, GROUPS)
        squares_sum = group_sums(feat_float * feat_float, GROUPS)
        average = totals / count_group
        inverse = lax.rsqrt(squares_sum / count_group - average * average + EPS_GROUP)
        normed = (feat_float - spread_groups(average, C)) * spread_groups(inverse, C)
        scaled = normed * gn_gain
        active, slope_silu = silu_parts(scaled)
        active = active.astype(jnp.bfloat16)
        rim_rows = jnp.pad(active, ((0, 0), (1, 1), (0, 0), (0, 0)))
        picture = jnp.zeros((1, H, W, 3), jnp.float32)
        for half_idx in range(2):
            chan_slice = slice(half_idx * half_chan, (half_idx + 1) * half_chan)
            picture = picture + round_half(conv_forward(rim_rows[..., chan_slice], conv_w[..., chan_slice]))
        picture = picture.astype(jnp.bfloat16)[0]
        patches = to_patches(picture)
        embedded = jnp.dot(patches, patch_w.T, preferred_element_type=jnp.float32) + pos_emb.astype(jnp.float32)
        normed_in, hat_in, inv_in = layer_norm(embedded, ln1_gain)
        normed_round = normed_in.astype(jnp.bfloat16)
        mixed_out = jnp.zeros((TOKENS, D), jnp.float32)
        stored = []
        for half_idx in range(2):
            col_slice = slice(half_idx * half_heads, (half_idx + 1) * half_heads)
            queries = jnp.dot(normed_round, qkv_flat[:, 0, col_slice], preferred_element_type=jnp.float32).astype(jnp.bfloat16)
            key_rows = jnp.dot(normed_round, qkv_flat[:, 1, col_slice], preferred_element_type=jnp.float32).astype(jnp.bfloat16)
            value_rows = jnp.dot(normed_round, qkv_flat[:, 2, col_slice], preferred_element_type=jnp.float32).astype(jnp.bfloat16)
            attended = attend(queries, key_rows, value_rows)
            mixed_out = mixed_out + round_half(jnp.dot(attended, out_flat[:, col_slice].T, preferred_element_type=jnp.float32))
            stored.append((queries, key_rows, value_rows))
        residual_out = embedded + mixed_out
        pooled = lax.optimization_barrier(jnp.mean(residual_out, axis=0))
        pooled_out, hat_z, inv_z = layer_norm(pooled, final_gain)
        reward = jnp.sum(pooled_out * head_w)
        upstream = layer_norm_back(head_w, hat_z, inv_z, final_gain)
        row_round = upstream.astype(jnp.bfloat16)[None, :]
        dnormed = jnp.zeros((TOKENS, D), jnp.float32)
        for half_idx in range(2):
            col_slice = slice(half_idx * half_heads, (half_idx + 1) * half_heads)
            queries, key_rows, value_rows = stored[half_idx]
            head_grad = jnp.dot(row_round, out_flat[:, col_slice], preferred_element_type=jnp.float32).astype(jnp.bfloat16)
            head_grad = jnp.broadcast_to(head_grad, queries.shape)
            dquery, dkey, dvalue = attend_back(queries, key_rows, value_rows, head_grad)
            partial_value = jnp.dot(dquery, qkv_flat[:, 0, col_slice].T, preferred_element_type=jnp.float32)
            partial_value = partial_value + jnp.dot(dkey, qkv_flat[:, 1, col_slice].T, preferred_element_type=jnp.float32)
            partial_value = partial_value + jnp.dot(dvalue, qkv_flat[:, 2, col_slice].T, preferred_element_type=jnp.float32)
            dnormed = dnormed + round_half(partial_value)
        dembedded = upstream[None, :] + layer_norm_back(dnormed, hat_in, inv_in, ln1_gain)
        dpatches = jnp.dot(dembedded.astype(jnp.bfloat16), patch_w, preferred_element_type=jnp.float32)
        dpicture = from_patches(dpatches, H, W).astype(jnp.bfloat16)
        grad_rim = jnp.pad(dpicture[None], ((0, 0), (1, 1), (0, 0), (0, 0)))
        dactive = conv_back(grad_rim, conv_w)
        gated_grad = dactive * slope_silu * gn_gain
        back_one = group_sums(gated_grad, GROUPS) / count_group
        back_two = group_sums(gated_grad * normed, GROUPS) / count_group
        grad_one = spread_groups(inverse, C) * (gated_grad - spread_groups(back_one, C) - normed * spread_groups(back_two, C))
        return (reward, grad_one[0].astype(jnp.bfloat16))
    rewards, grad_maps = lax.map(one_image, feat_maps)
    grad_features = grad_maps.reshape(IMAGES, H, W, 2, HALF_C).transpose(0, 1, 3, 2, 4).reshape(IMAGES, H, 2, W * HALF_C)
    group_base = jnp.arange(IMAGES, dtype=jnp.int32) // IMG_SLAB * IMG_SLAB
    slot_index = (owner_slot.reshape(IMAGES).astype(jnp.int32) + group_base).astype(jnp.int32)
    slot_reward = jnp.zeros_like(rewards).at[slot_index].set(rewards)
    return (grad_features, slot_reward)
```

```python
import functools
import math

import jax
import jax.numpy as jnp
from jax import lax
from jax.experimental import pallas as pl
from jax.experimental.pallas import tpu as pltpu
from jax.sharding import PartitionSpec as P

C = 128
GROUPS = 32
PATCH = 14
HEAD_DIM = 80
W = 112


EPS_GROUP = 1e-06
EPS_LAYER = 1e-05


def exchange_kernel(axes, sizes, pick, x_ref, o_ref, send_sems, recv_sems, local_sem):
    total = math.prod(sizes)
    me = 0
    for axis, size in zip(axes, sizes):
        me = me * size + lax.axis_index(axis)

    def place(offset):
        index = lax.rem(me + offset, total)
        rest = index
        where = {}
        for axis, size in reversed(list(zip(axes, sizes))):
            where[axis] = lax.rem(rest, size)
            rest = rest // size
        return index, where

    def chunk(index):
        return x_ref if pick is None else x_ref.at[index // pick]

    barrier = pltpu.get_barrier_semaphore()
    for offset in range(1, total):
        pl.semaphore_signal(
            barrier, inc=1, device_id=place(offset)[1], device_id_type=pl.DeviceIdType.MESH
        )
    own = pltpu.make_async_copy(chunk(me), o_ref.at[me], local_sem)
    own.start()
    pl.semaphore_wait(barrier, total - 1)
    copies = []
    for offset in range(1, total):
        index, where = place(offset)
        copy = pltpu.make_async_remote_copy(
            src_ref=chunk(index),
            dst_ref=o_ref.at[me],
            send_sem=send_sems.at[offset - 1],
            recv_sem=recv_sems.at[offset - 1],
            device_id=where,
            device_id_type=pl.DeviceIdType.MESH,
        )
        copy.start()
        copies.append(copy)
    own.wait()
    for copy in copies:
        copy.wait()


def exchange(values, axes, pick, ident):
    sizes = tuple(lax.axis_size(axis) for axis in axes)
    total = math.prod(sizes)
    item = values.shape if pick is None else values.shape[1:]
    size_out = total * math.prod(item) * values.dtype.itemsize
    space = pltpu.VMEM if size_out <= 4 * 2**20 else pl.ANY
    return pl.pallas_call(
        functools.partial(exchange_kernel, axes, sizes, pick),
        out_shape=jax.ShapeDtypeStruct((total,) + item, values.dtype),
        in_specs=[pl.BlockSpec(memory_space=space)],
        out_specs=pl.BlockSpec(memory_space=space),
        scratch_shapes=[
            pltpu.SemaphoreType.DMA((total - 1,)),
            pltpu.SemaphoreType.DMA((total - 1,)),
            pltpu.SemaphoreType.DMA,
        ],
        compiler_params=pltpu.CompilerParams(collective_id=ident, has_side_effects=True),
    )(values)


def round_half(values):
    return lax.optimization_barrier(values.astype(jnp.bfloat16)).astype(jnp.float32)


def layer_norm(values, scale_vec):
    average = jnp.mean(values, axis=-1, keepdims=True)
    centred = values - average
    spread = jnp.mean(centred * centred, axis=-1, keepdims=True)
    inverse = lax.rsqrt(spread + EPS_LAYER)
    normed = centred * inverse
    return (normed * scale_vec, normed, inverse)


def layer_norm_back(upstream, normed, inverse, scale_vec):
    scaled = upstream * scale_vec
    mean_one = jnp.mean(scaled, axis=-1, keepdims=True)
    mean_two = jnp.mean(scaled * normed, axis=-1, keepdims=True)
    return inverse * (scaled - mean_one - normed * mean_two)


def silu_parts(values):
    sigmoid = jax.nn.sigmoid(values)
    return (values * sigmoid, sigmoid * (1.0 + values * (1.0 - sigmoid)))


def fill(values, sizes):
    return jnp.pad(values, [(0, size - have) for size, have in zip(sizes, values.shape)])


def up16(count):
    return (count + 15) // 16 * 16


def attention(queries, key_rows):
    factor = 1.0 / math.sqrt(HEAD_DIM)
    scores = jnp.einsum("bthd,bshd->bhts", queries, key_rows, preferred_element_type=jnp.float32)
    scores = scores * factor
    row_max = jnp.max(scores, axis=-1, keepdims=True)
    exp_scores = jnp.exp(scores - row_max)
    return exp_scores / jnp.sum(exp_scores, axis=-1, keepdims=True)


def body(
    features,
    gn_gain,
    conv_w,
    patch_w,
    pos_emb,
    ln1_gain,
    qkv_w,
    out_w,
    final_gain,
    head_w,
    owner_slot,
):
    slab_imgs, rows_here, _, flat_width = features.shape
    col_count = W
    chan_count = flat_width // col_count
    row_devices = lax.axis_size("rows")
    rows_total = rows_here * row_devices
    groups_here = GROUPS * chan_count // C
    group_width = chan_count // groups_here
    count_group = rows_total * col_count * group_width
    half_patch = PATCH // 2
    patch_rows = rows_total // half_patch
    patch_cols = col_count // half_patch

    tp_devices = lax.axis_size("tp")
    feat_own, _, half_width = qkv_w.shape
    width = pos_emb.shape[1]
    heads_half = half_width // HEAD_DIM
    split_axes = ("grp", "img")
    if heads_half % (lax.axis_size("grp") * lax.axis_size("img")):
        split_axes = ("img",)
    planes = math.prod(lax.axis_size(axis) for axis in split_axes)
    plane_index = 0
    for axis in split_axes:
        plane_index = plane_index * lax.axis_size(axis) + lax.axis_index(axis)
    heads_mine = heads_half // planes
    span = heads_mine * HEAD_DIM
    cell_entries = 3 * half_patch * half_patch
    entry_index = jnp.arange(3 * PATCH * PATCH, dtype=jnp.int32)
    pixel_index = entry_index // 3
    target = (
        entry_index % 3 * half_patch * half_patch
        + pixel_index // PATCH // 2 * half_patch
        + pixel_index % PATCH // 2
    )
    fold_table = (
        target[:, None] == jnp.arange(cell_entries, dtype=jnp.int32)[None, :]
    ).astype(jnp.bfloat16)
    folded_own = jnp.dot(patch_w, fold_table, preferred_element_type=jnp.float32)
    weights_own = jnp.concatenate(
        [
            lax.dynamic_slice_in_dim(qkv_w, plane_index * span, span, 2).reshape(feat_own, 3 * span),
            lax.dynamic_slice_in_dim(out_w, plane_index * span, span, 1),
            folded_own.astype(jnp.bfloat16),
        ],
        axis=1,
    )
    weights_wide = (4 * span + cell_entries + 127) // 128 * 128
    weights = lax.all_gather(
        fill(weights_own, (feat_own, weights_wide)), "rows", axis=0, tiled=True
    )
    qkv_cols = weights[:, : 3 * span]
    out_cols = weights[:, 3 * span : 4 * span]
    folded_weight = weights[:, 4 * span : 4 * span + cell_entries]

    def channel_group_sums(flat):
        per_col = jnp.sum(flat, axis=1).reshape(slab_imgs, col_count, chan_count)
        per_chan = jnp.sum(per_col, axis=1)
        return jnp.sum(per_chan.reshape(slab_imgs, groups_here, group_width), axis=2)

    def rows_total_sum(values, ident):
        flat = fill(values.reshape(2 * slab_imgs, groups_here), (2 * slab_imgs, 128))
        summed = jnp.sum(exchange(flat, ("rows",), None, ident), axis=0)
        return summed[:, :groups_here].reshape(2, slab_imgs, groups_here)

    def spread_flat(per_group):
        return jnp.tile(jnp.repeat(per_group, group_width, axis=1), (1, col_count))[:, None, :]

    feat_float = features.reshape(slab_imgs, rows_here, flat_width).astype(jnp.float32)
    stat_sums = rows_total_sum(
        jnp.stack([channel_group_sums(feat_float), channel_group_sums(feat_float * feat_float)]), 1
    )
    average = stat_sums[0] / count_group
    inverse = lax.rsqrt(stat_sums[1] / count_group - average * average + EPS_GROUP)
    gain_flat = jnp.tile(gn_gain, col_count)[None, None, :]
    normed = (feat_float - spread_flat(average)) * spread_flat(inverse)
    scaled = normed * gain_flat
    active, slope_silu = silu_parts(scaled)
    active = active.astype(jnp.bfloat16)
    kernel_rows = conv_w.reshape(27, chan_count)
    widened = jnp.pad(active, ((0, 0), (2, 2), (0, 0)))
    block_rows = widened.shape[1]
    padded = jnp.pad(widened, ((0, 0), (0, 0), (chan_count, chan_count)))
    terms = lax.dot_general(
        kernel_rows,
        padded.reshape(-1, chan_count),
        (((1,), (1,)), ((), ())),
        preferred_element_type=jnp.float32,
    )
    shifted_terms = terms.reshape(3, 3, 3, slab_imgs, block_rows, col_count + 2)
    out_rows = rows_here + 2
    total = jnp.zeros((3, slab_imgs, out_rows, col_count), jnp.float32)
    for shifted_offset_y in range(3):
        for shifted_offset_x in range(3):
            total = (
                total
                + shifted_terms[
                    :,
                    shifted_offset_y,
                    shifted_offset_x,
                    :,
                    shifted_offset_y : shifted_offset_y + out_rows,
                    shifted_offset_x : shifted_offset_x + col_count,
                ]
            )
    mine = lax.axis_index("rows")
    tokens = patch_rows * patch_cols
    rim_entries = 3 * out_rows
    slot_of = owner_slot[0]
    slot_ids = jnp.arange(slab_imgs, dtype=jnp.int32)
    selector = (slot_of[None, :] == slot_ids[:, None]).astype(jnp.bfloat16)
    partial = total.transpose(1, 0, 2, 3).reshape(slab_imgs, -1).astype(jnp.bfloat16)
    ordered = jnp.dot(selector, partial, preferred_element_type=jnp.float32).astype(jnp.bfloat16)
    ordered = ordered.reshape(slab_imgs, rim_entries, col_count)
    slabs = exchange(
        fill(ordered, (slab_imgs, up16(rim_entries), 128)),
        ("rows",) + split_axes + ("tp",),
        planes * tp_devices,
        2,
    )
    slabs = slabs[:, :rim_entries, :col_count].astype(jnp.float32)
    slabs = slabs.reshape(row_devices, planes, tp_devices, 3, out_rows, col_count)
    slabs = jnp.sum(slabs, axis=2)
    middle = slabs[:, :, :, 1:-1]
    above = jnp.pad(slabs[:-1, :, :, -1:], ((1, 0), (0, 0), (0, 0), (0, rows_here - 1), (0, 0)))
    below = jnp.pad(slabs[1:, :, :, :1], ((0, 1), (0, 0), (0, 0), (rows_here - 1, 0), (0, 0)))
    picture = (middle + above + below).astype(jnp.bfloat16)

    patch_cells = picture.reshape(
        patch_rows, planes, 3, half_patch, patch_cols, half_patch
    ).transpose(1, 0, 4, 2, 3, 5)
    patch_cells = patch_cells.reshape(planes * tokens, cell_entries)
    embedded = lax.dot_general(
        patch_cells, folded_weight, (((1,), (1,)), ((), ())), preferred_element_type=jnp.float32
    ).reshape(planes, tokens, width) + pos_emb.astype(jnp.float32)
    normed_in, hat_in, inv_in = layer_norm(embedded, ln1_gain)
    pooled_in = jnp.mean(embedded, axis=1)
    qkv = jnp.dot(
        normed_in.astype(jnp.bfloat16).reshape(planes * tokens, width),
        qkv_cols,
        preferred_element_type=jnp.float32,
    ).astype(jnp.bfloat16)
    qkv = qkv.reshape(planes, tokens, 3, heads_mine, HEAD_DIM)
    queries, key_rows, value_rows = qkv[:, :, 0], qkv[:, :, 1], qkv[:, :, 2]
    prob_soft = attention(queries, key_rows)
    prob_columns = jnp.sum(round_half(prob_soft), axis=2)
    value_float = value_rows.astype(jnp.float32)
    attended_mean = jnp.sum(
        (prob_columns / tokens).transpose(0, 2, 1)[..., None] * value_float, axis=1
    ).reshape(planes, span)
    attended_high = attended_mean.astype(jnp.bfloat16)
    attended_low = (attended_mean - attended_high.astype(jnp.float32)).astype(jnp.bfloat16)
    mixed = lax.dot_general(
        jnp.stack([attended_high, attended_low]).reshape(2 * planes, span),
        out_cols,
        (((1,), (1,)), ((), ())),
        preferred_element_type=jnp.float32,
    )
    mixed = jnp.sum(mixed.reshape(2, planes, width), axis=0)
    mixed = jnp.sum(exchange(mixed, split_axes + ("tp",), None, 3), axis=0)
    pooled_out, hat_z, inv_z = layer_norm(pooled_in + mixed, final_gain)
    rewards = jnp.sum(pooled_out * head_w, axis=-1)
    rewards = lax.dynamic_slice_in_dim(rewards, plane_index, 1)
    upstream = layer_norm_back(head_w, hat_z, inv_z, final_gain)
    head_grad = (
        jnp.dot(upstream.astype(jnp.bfloat16), out_cols, preferred_element_type=jnp.float32)
        .astype(jnp.bfloat16)
        .astype(jnp.float32)
        .reshape(planes, 1, heads_mine, HEAD_DIM)
    )
    dprob = jnp.sum(head_grad * value_float, axis=-1).transpose(0, 2, 1)[:, :, None, :]
    factor = 1.0 / math.sqrt(HEAD_DIM)
    dscores = prob_soft * (dprob - jnp.sum(dprob * prob_soft, axis=-1, keepdims=True)) * factor
    dscores = dscores.astype(jnp.bfloat16)
    dvalue = (prob_columns.transpose(0, 2, 1)[..., None] * head_grad).astype(jnp.bfloat16)
    dquery = jnp.einsum(
        "bhts,bshd->bthd", dscores, key_rows, preferred_element_type=jnp.float32
    ).astype(jnp.bfloat16)
    dkey = jnp.einsum(
        "bhts,bthd->bshd", dscores, queries, preferred_element_type=jnp.float32
    ).astype(jnp.bfloat16)
    dqkv = jnp.stack([dquery, dkey, dvalue], axis=2).reshape(planes * tokens, 3 * span)
    dnormed = lax.dot_general(
        dqkv, qkv_cols, (((1,), (1,)), ((), ())), preferred_element_type=jnp.float32
    ).reshape(planes, tokens, width)
    first = jnp.where(plane_index + lax.axis_index("tp") == 0, 1.0, 0.0)
    dembedded = (upstream * first)[:, None, :] + layer_norm_back(dnormed, hat_in, inv_in, ln1_gain)
    cell_grads = jnp.dot(
        dembedded.astype(jnp.bfloat16).reshape(planes * tokens, width),
        folded_weight,
        preferred_element_type=jnp.float32,
    ).astype(jnp.bfloat16)
    cell_grads = cell_grads.reshape(
        planes, patch_rows, patch_cols, 3, half_patch, half_patch
    ).transpose(0, 3, 1, 4, 2, 5)
    back_image = jnp.pad(
        cell_grads.reshape(planes, 3, rows_total, col_count), ((0, 0), (0, 0), (1, 1), (0, 0))
    )
    slabs_back = jnp.stack(
        [back_image[:, :, r * rows_here : r * rows_here + out_rows] for r in range(row_devices)]
    ).reshape(row_devices * planes, rim_entries, col_count)
    returned = exchange(
        fill(slabs_back, (row_devices * planes, up16(rim_entries), 128)),
        ("rows",) + split_axes + ("tp",),
        tp_devices,
        4,
    )
    returned = returned[:, :rim_entries, :col_count].astype(jnp.float32)
    by_slot = jnp.sum(
        returned.reshape(row_devices, planes * tp_devices, rim_entries * col_count), axis=1
    ).astype(jnp.bfloat16)
    dpicture = jnp.dot(selector.T, by_slot, preferred_element_type=jnp.float32).astype(jnp.bfloat16)
    grad_rimmed = dpicture.reshape(slab_imgs, 3, out_rows, col_count).transpose(1, 0, 2, 3)
    grad_padded = jnp.pad(grad_rimmed, ((0, 0), (0, 0), (0, 0), (1, 1)))
    windows = []
    for offset_y in range(3):
        for offset_x in range(3):
            windows.append(
                grad_padded[
                    :,
                    :,
                    2 - offset_y : 2 - offset_y + rows_here,
                    2 - offset_x : 2 - offset_x + col_count,
                ]
            )
    stacked = jnp.stack(windows, axis=1).reshape(27, -1)
    dactive = lax.dot_general(
        stacked, kernel_rows, (((0,), (0,)), ((), ())), preferred_element_type=jnp.float32
    )
    dactive = dactive.reshape(slab_imgs, rows_here, flat_width)
    gated_grad = dactive * slope_silu * gain_flat
    back_sums = rows_total_sum(
        jnp.stack([channel_group_sums(gated_grad), channel_group_sums(gated_grad * normed)]), 5
    )
    back_one = back_sums[0] / count_group
    back_two = back_sums[1] / count_group
    grad_features = spread_flat(inverse) * (
        gated_grad - spread_flat(back_one) - normed * spread_flat(back_two)
    )
    grad_out = grad_features.astype(jnp.bfloat16).reshape(slab_imgs, rows_here, 1, flat_width)
    return (grad_out, rewards)


def solution(mesh):
    placed = (
        P(("grp", "img"), "rows", "tp", None),
        P("tp"),
        P(None, None, None, "tp"),
        P("rows", None),
        P(),
        P(),
        P("rows", None, "tp"),
        P("rows", "tp"),
        P(),
        P(),
        P(("grp", "img"), None),
    )
    return jax.shard_map(
        body,
        mesh=mesh,
        in_specs=placed,
        out_specs=(P(("grp", "img"), "rows", "tp", None), P(("grp", "img", "rows"))),
        check_vma=False,
    )
```

```python
import functools
import math

import jax
import jax.numpy as jnp
from jax import lax
from jax.experimental import pallas as pl
from jax.experimental.pallas import tpu as pltpu
from jax.sharding import PartitionSpec as P

C = 128
GROUPS = 32
PATCH = 14
HEAD_DIM = 80
W = 112


EPS_GROUP = 1e-06
EPS_LAYER = 1e-05


def exchange_kernel(axes, sizes, pick, x_ref, o_ref, send_sems, recv_sems, local_sem):
    total = math.prod(sizes)
    me = 0
    for axis, size in zip(axes, sizes):
        me = me * size + lax.axis_index(axis)

    def place(offset):
        index = lax.rem(me + offset, total)
        rest = index
        where = {}
        for axis, size in reversed(list(zip(axes, sizes))):
            where[axis] = lax.rem(rest, size)
            rest = rest // size
        return index, where

    def chunk(index):
        return x_ref if pick is None else x_ref.at[index // pick]

    barrier = pltpu.get_barrier_semaphore()
    for offset in range(1, total):
        pl.semaphore_signal(
            barrier, inc=1, device_id=place(offset)[1], device_id_type=pl.DeviceIdType.MESH
        )
    own = pltpu.make_async_copy(chunk(me), o_ref.at[me], local_sem)
    own.start()
    pl.semaphore_wait(barrier, total - 1)
    copies = []
    for offset in range(1, total):
        index, where = place(offset)
        copy = pltpu.make_async_remote_copy(
            src_ref=chunk(index),
            dst_ref=o_ref.at[me],
            send_sem=send_sems.at[offset - 1],
            recv_sem=recv_sems.at[offset - 1],
            device_id=where,
            device_id_type=pl.DeviceIdType.MESH,
        )
        copy.start()
        copies.append(copy)
    own.wait()
    for copy in copies:
        copy.wait()


def exchange(values, axes, pick, ident):
    sizes = tuple(lax.axis_size(axis) for axis in axes)
    total = math.prod(sizes)
    item = values.shape if pick is None else values.shape[1:]
    size_out = total * math.prod(item) * values.dtype.itemsize
    space = pltpu.VMEM if size_out <= 4 * 2**20 else pl.ANY
    return pl.pallas_call(
        functools.partial(exchange_kernel, axes, sizes, pick),
        out_shape=jax.ShapeDtypeStruct((total,) + item, values.dtype),
        in_specs=[pl.BlockSpec(memory_space=space)],
        out_specs=pl.BlockSpec(memory_space=space),
        scratch_shapes=[
            pltpu.SemaphoreType.DMA((total - 1,)),
            pltpu.SemaphoreType.DMA((total - 1,)),
            pltpu.SemaphoreType.DMA,
        ],
        compiler_params=pltpu.CompilerParams(collective_id=ident, has_side_effects=True),
    )(values)


def round_half(values):
    return lax.optimization_barrier(values.astype(jnp.bfloat16)).astype(jnp.float32)


def layer_norm(values, scale_vec):
    average = jnp.mean(values, axis=-1, keepdims=True)
    centred = values - average
    spread = jnp.mean(centred * centred, axis=-1, keepdims=True)
    inverse = lax.rsqrt(spread + EPS_LAYER)
    normed = centred * inverse
    return (normed * scale_vec, normed, inverse)


def layer_norm_back(upstream, normed, inverse, scale_vec):
    scaled = upstream * scale_vec
    mean_one = jnp.mean(scaled, axis=-1, keepdims=True)
    mean_two = jnp.mean(scaled * normed, axis=-1, keepdims=True)
    return inverse * (scaled - mean_one - normed * mean_two)


def silu_parts(values):
    sigmoid = jax.nn.sigmoid(values)
    return (values * sigmoid, sigmoid * (1.0 + values * (1.0 - sigmoid)))


def fill(values, sizes):
    return jnp.pad(values, [(0, size - have) for size, have in zip(sizes, values.shape)])


def up16(count):
    return (count + 15) // 16 * 16


def mm(left, right, left_dim, right_dim):
    return lax.dot_general(
        left, right, (((left_dim,), (right_dim,)), ((), ())), preferred_element_type=jnp.float32
    )


def hold(values):
    return values.astype(jnp.bfloat16)


class Windows:
    def __init__(self, span, heads_mine, cell_entries):
        self.fold = (cell_entries + 127) // 128 * 128
        self.heads = heads_mine
        end = self.fold + 3 * span
        self.wide = (end + span + 127) // 128 * 128
        self.high = (end + 127) // 128 * 128
        self.low = end // 128 * 128
        self.end = end

    def select(self, start, stop, first, blocks):
        row = jnp.arange(start, stop, dtype=jnp.int32)[:, None]
        column = jnp.arange(blocks * 128, dtype=jnp.int32)[None, :]
        lane = column % 128
        hit = (row == first + column // 128 * HEAD_DIM + lane) & (lane < HEAD_DIM)
        return hit.astype(jnp.bfloat16)


def over(count, step):
    if count == 1:
        step(0)
    else:

        @pl.loop(0, count)
        def _(index):
            step(index)


def scorer_forward(
    win, planes, tokens, per_chunk, cells_ref, w_ref, pick_qkv_ref, pick_out_ref, pos_ref, gain_ref,
    hat_ref, inv_ref, heads_ref, prob_ref, mixed_ref, pooled_ref, att_ref,
):
    heads = win.heads
    rows = per_chunk * tokens
    factor = 1.0 / math.sqrt(HEAD_DIM)

    def embed(index):
        at = pl.ds(pl.multiple_of(index * rows, rows), rows)
        embedded = mm(cells_ref[at, :], w_ref[:, : win.fold], 1, 1)
        width = embedded.shape[1]
        embedded = embedded.reshape(per_chunk, tokens, width) + pos_ref[...].astype(jnp.float32)[None]
        for inner in range(per_chunk):
            pooled_ref[pl.ds(index * per_chunk + inner, 1), :] = jnp.mean(
                embedded[inner], axis=0, keepdims=True
            )
        embedded = embedded.reshape(rows, width)
        normed_in, hat, inverse = layer_norm(embedded, gain_ref[...])
        hat_ref[at, :] = hat
        inv_ref[at, :] = jnp.broadcast_to(inverse, (rows, 128))
        flat = hold(mm(hold(normed_in), w_ref[:, win.fold : win.high], 1, 0))
        heads_ref[at, :] = hold(mm(flat, pick_qkv_ref[...], 1, 0))

    over(planes // per_chunk, embed)

    def attend(plane):
        at = pl.ds(pl.multiple_of(plane * tokens, tokens), tokens)
        for head in range(heads):
            query = heads_ref[at, head * 128 : head * 128 + 128]
            key = heads_ref[at, (heads + head) * 128 : (heads + head) * 128 + 128]
            value = heads_ref[at, (2 * heads + head) * 128 : (2 * heads + head) * 128 + 128]
            scores = mm(query, key, 1, 1) * factor
            exp_scores = jnp.exp(scores - jnp.max(scores, axis=-1, keepdims=True))
            prob = exp_scores / jnp.sum(exp_scores, axis=-1, keepdims=True)
            prob_ref[at, head * tokens : head * tokens + tokens] = prob
            mean_row = (
                jnp.sum(hold(prob).astype(jnp.float32), axis=0, keepdims=True) * (1.0 / tokens)
            )
            mean_high = hold(mean_row)
            mean_low = hold(mean_row - mean_high.astype(jnp.float32))
            att_ref[pl.ds(plane, 1), head * 128 : head * 128 + 128] = mm(
                mean_high, value, 1, 0
            ) + mm(mean_low, value, 1, 0)

    if planes * heads <= 8 and tokens <= 64:
        for plane in range(planes):
            attend(plane)
    else:
        over(planes, attend)
    attended = att_ref[...]
    high = hold(attended)
    low = hold(attended - high.astype(jnp.float32))
    out_window = w_ref[:, win.low :]
    mixed_ref[...] = mm(hold(mm(high, pick_out_ref[...], 1, 1)), out_window, 1, 1) + mm(
        hold(mm(low, pick_out_ref[...], 1, 1)), out_window, 1, 1
    )


def scorer_backward(
    win, planes, tokens, per_chunk, mixed_ref, pooled_ref, final_ref, head_w_ref, first_ref, w_ref,
    pick_qkv_ref, pick_out_ref, gain_ref, hat_ref, inv_ref, heads_ref, prob_ref,
    dcells_ref, reward_ref, grad_ref, up_ref, share_ref,
):
    heads = win.heads
    rows = per_chunk * tokens
    factor = 1.0 / math.sqrt(HEAD_DIM)
    pooled = pooled_ref[...]
    for index in range(mixed_ref.shape[0]):
        pooled = pooled + mixed_ref[index]
    final_gain = final_ref[...]
    head_w = head_w_ref[...]
    pooled_out, hat_z, inv_z = layer_norm(pooled, final_gain)
    reward_ref[...] = jnp.broadcast_to(
        jnp.sum(pooled_out * head_w, axis=-1, keepdims=True), reward_ref.shape
    )
    upstream = layer_norm_back(head_w, hat_z, inv_z, final_gain)
    up_ref[...] = upstream * first_ref[0:1, 0:1]
    share_ref[...] = mm(
        hold(mm(hold(upstream), w_ref[:, win.low :], 1, 0)), pick_out_ref[...], 1, 0
    )

    def attend(plane):
        at = pl.ds(pl.multiple_of(plane * tokens, tokens), tokens)
        for head in range(heads):
            lanes = [
                slice((which * heads + head) * 128, (which * heads + head) * 128 + 128)
                for which in range(3)
            ]
            query, key, value = (heads_ref[at, lane] for lane in lanes)
            prob = prob_ref[at, head * tokens : head * tokens + tokens]
            share = hold(
                jnp.broadcast_to(
                    share_ref[pl.ds(plane, 1), head * 128 : head * 128 + 128], (tokens, 128)
                )
            )
            dprob = mm(share, value, 1, 1)
            dscores = hold(
                prob * (dprob - jnp.sum(dprob * prob, axis=-1, keepdims=True)) * factor
            )
            grad_ref[at, lanes[0]] = hold(mm(dscores, key, 1, 0))
            grad_ref[at, lanes[1]] = hold(mm(dscores, query, 0, 0))
            grad_ref[at, lanes[2]] = hold(mm(hold(prob), share, 0, 0))

    if planes * heads <= 8 and tokens <= 64:
        for plane in range(planes):
            attend(plane)
    else:
        over(planes, attend)

    def finish(index):
        at = pl.ds(pl.multiple_of(index * rows, rows), rows)
        flat = hold(mm(grad_ref[at, :], pick_qkv_ref[...], 1, 1))
        dnormed = mm(flat, w_ref[:, win.fold : win.high], 1, 1)
        dlinear = layer_norm_back(dnormed, hat_ref[at, :], inv_ref[at, 0:1], gain_ref[...])
        width = dlinear.shape[1]
        dlinear = dlinear.reshape(per_chunk, tokens, width)
        pieces = [
            dlinear[inner] + up_ref[pl.ds(index * per_chunk + inner, 1), :]
            for inner in range(per_chunk)
        ]
        dembedded = hold(jnp.concatenate(pieces, axis=0) if per_chunk > 1 else pieces[0])
        dcells_ref[at, :] = hold(mm(dembedded, w_ref[:, : win.fold], 1, 0))

    over(planes // per_chunk, finish)


def local_call(kernel, shapes, scratch, *operands):
    vmem = pl.BlockSpec(memory_space=pltpu.VMEM)
    return pl.pallas_call(
        kernel,
        out_shape=shapes,
        in_specs=[vmem] * len(operands),
        out_specs=[vmem] * len(shapes),
        scratch_shapes=scratch,
        compiler_params=pltpu.CompilerParams(vmem_limit_bytes=56 * 2**20),
    )(*operands)


def body(
    features,
    gn_gain,
    conv_w,
    patch_w,
    pos_emb,
    ln1_gain,
    qkv_w,
    out_w,
    final_gain,
    head_w,
    owner_slot,
):
    slab_imgs, rows_here, _, flat_width = features.shape
    col_count = W
    chan_count = flat_width // col_count
    row_devices = lax.axis_size("rows")
    rows_total = rows_here * row_devices
    groups_here = GROUPS * chan_count // C
    group_width = chan_count // groups_here
    count_group = rows_total * col_count * group_width
    half_patch = PATCH // 2
    patch_rows = rows_total // half_patch
    patch_cols = col_count // half_patch

    tp_devices = lax.axis_size("tp")
    feat_own, _, half_width = qkv_w.shape
    width = pos_emb.shape[1]
    heads_half = half_width // HEAD_DIM
    split_axes = ("grp", "img")
    if heads_half % (lax.axis_size("grp") * lax.axis_size("img")):
        split_axes = ("img",)
    planes = math.prod(lax.axis_size(axis) for axis in split_axes)
    plane_index = 0
    for axis in split_axes:
        plane_index = plane_index * lax.axis_size(axis) + lax.axis_index(axis)
    heads_mine = heads_half // planes
    span = heads_mine * HEAD_DIM
    cell_entries = 3 * half_patch * half_patch
    entry_index = jnp.arange(3 * PATCH * PATCH, dtype=jnp.int32)
    pixel_index = entry_index // 3
    target = (
        entry_index % 3 * half_patch * half_patch
        + pixel_index // PATCH // 2 * half_patch
        + pixel_index % PATCH // 2
    )
    fold_table = (
        target[:, None] == jnp.arange(cell_entries, dtype=jnp.int32)[None, :]
    ).astype(jnp.bfloat16)
    folded_own = jnp.dot(patch_w, fold_table, preferred_element_type=jnp.float32)
    win = Windows(span, heads_mine, cell_entries)
    weights_own = jnp.concatenate(
        [
            fill(folded_own.astype(jnp.bfloat16), (feat_own, win.fold)),
            lax.dynamic_slice_in_dim(qkv_w, plane_index * span, span, 2).reshape(feat_own, 3 * span),
            lax.dynamic_slice_in_dim(out_w, plane_index * span, span, 1),
        ],
        axis=1,
    )
    weights = lax.all_gather(fill(weights_own, (feat_own, win.wide)), "rows", axis=0, tiled=True)
    pick_qkv = win.select(win.fold, win.high, win.fold, 3 * heads_mine)
    pick_out = win.select(win.low, win.wide, win.end, heads_mine)

    def channel_group_sums(flat):
        per_col = jnp.sum(flat, axis=1).reshape(slab_imgs, col_count, chan_count)
        per_chan = jnp.sum(per_col, axis=1)
        return jnp.sum(per_chan.reshape(slab_imgs, groups_here, group_width), axis=2)

    def rows_total_sum(values, ident):
        flat = fill(values.reshape(2 * slab_imgs, groups_here), (2 * slab_imgs, 128))
        summed = jnp.sum(exchange(flat, ("rows",), None, ident), axis=0)
        return summed[:, :groups_here].reshape(2, slab_imgs, groups_here)

    def spread_flat(per_group):
        return jnp.tile(jnp.repeat(per_group, group_width, axis=1), (1, col_count))[:, None, :]

    feat_float = features.reshape(slab_imgs, rows_here, flat_width).astype(jnp.float32)
    stat_sums = rows_total_sum(
        jnp.stack([channel_group_sums(feat_float), channel_group_sums(feat_float * feat_float)]), 1
    )
    average = stat_sums[0] / count_group
    inverse = lax.rsqrt(stat_sums[1] / count_group - average * average + EPS_GROUP)
    gain_flat = jnp.tile(gn_gain, col_count)[None, None, :]
    normed = (feat_float - spread_flat(average)) * spread_flat(inverse)
    scaled = normed * gain_flat
    active, slope_silu = silu_parts(scaled)
    active = active.astype(jnp.bfloat16)
    kernel_rows = conv_w.reshape(27, chan_count)
    widened = jnp.pad(active, ((0, 0), (2, 2), (0, 0)))
    block_rows = widened.shape[1]
    padded = jnp.pad(widened, ((0, 0), (0, 0), (chan_count, chan_count)))
    terms = lax.dot_general(
        kernel_rows,
        padded.reshape(-1, chan_count),
        (((1,), (1,)), ((), ())),
        preferred_element_type=jnp.float32,
    )
    shifted_terms = terms.reshape(3, 3, 3, slab_imgs, block_rows, col_count + 2)
    out_rows = rows_here + 2
    total = jnp.zeros((3, slab_imgs, out_rows, col_count), jnp.float32)
    for shifted_offset_y in range(3):
        for shifted_offset_x in range(3):
            total = (
                total
                + shifted_terms[
                    :,
                    shifted_offset_y,
                    shifted_offset_x,
                    :,
                    shifted_offset_y : shifted_offset_y + out_rows,
                    shifted_offset_x : shifted_offset_x + col_count,
                ]
            )
    mine = lax.axis_index("rows")
    tokens = patch_rows * patch_cols
    rim_entries = 3 * out_rows
    slot_of = owner_slot[0]
    slot_ids = jnp.arange(slab_imgs, dtype=jnp.int32)
    selector = (slot_of[None, :] == slot_ids[:, None]).astype(jnp.bfloat16)
    partial = total.transpose(1, 0, 2, 3).reshape(slab_imgs, -1).astype(jnp.bfloat16)
    ordered = jnp.dot(selector, partial, preferred_element_type=jnp.float32).astype(jnp.bfloat16)
    ordered = ordered.reshape(slab_imgs, rim_entries, col_count)
    slabs = exchange(
        fill(ordered, (slab_imgs, up16(rim_entries), 128)),
        ("rows",) + split_axes + ("tp",),
        planes * tp_devices,
        2,
    )
    slabs = slabs[:, :rim_entries, :col_count].astype(jnp.float32)
    slabs = slabs.reshape(row_devices, planes, tp_devices, 3, out_rows, col_count)
    slabs = jnp.sum(slabs, axis=2)
    middle = slabs[:, :, :, 1:-1]
    above = jnp.pad(slabs[:-1, :, :, -1:], ((1, 0), (0, 0), (0, 0), (0, rows_here - 1), (0, 0)))
    below = jnp.pad(slabs[1:, :, :, :1], ((0, 1), (0, 0), (0, 0), (rows_here - 1, 0), (0, 0)))
    picture = (middle + above + below).astype(jnp.bfloat16)

    patch_cells = picture.reshape(
        patch_rows, planes, 3, half_patch, patch_cols, half_patch
    ).transpose(1, 0, 4, 2, 3, 5)
    patch_cells = patch_cells.reshape(planes * tokens, cell_entries)
    total_rows = planes * tokens
    per_chunk = max(1, min(planes, 256 // tokens))
    shape = jax.ShapeDtypeStruct
    gain_row = ln1_gain[None]
    hat_in, inv_in, head_cols, prob_soft, mixed, pooled_in = local_call(
        functools.partial(scorer_forward, win, planes, tokens, per_chunk),
        [
            shape((total_rows, width), jnp.float32),
            shape((total_rows, 128), jnp.float32),
            shape((total_rows, 3 * heads_mine * 128), jnp.bfloat16),
            shape((total_rows, heads_mine * tokens), jnp.float32),
            shape((planes, width), jnp.float32),
            shape((planes, width), jnp.float32),
        ],
        [pltpu.VMEM((planes, heads_mine * 128), jnp.float32)],
        fill(patch_cells, (total_rows, win.fold)),
        weights,
        pick_qkv,
        pick_out,
        pos_emb,
        gain_row,
    )
    mixed = exchange(mixed, split_axes + ("tp",), None, 3)
    first = jnp.where(plane_index + lax.axis_index("tp") == 0, 1.0, 0.0)
    cell_grads, rewards = local_call(
        functools.partial(scorer_backward, win, planes, tokens, per_chunk),
        [
            shape((total_rows, win.fold), jnp.bfloat16),
            shape((planes, 128), jnp.float32),
        ],
        [
            pltpu.VMEM((total_rows, 3 * heads_mine * 128), jnp.bfloat16),
            pltpu.VMEM((planes, width), jnp.float32),
            pltpu.VMEM((planes, heads_mine * 128), jnp.float32),
        ],
        mixed,
        pooled_in,
        final_gain[None],
        head_w[None],
        jnp.broadcast_to(first, (1, 128)),
        weights,
        pick_qkv,
        pick_out,
        gain_row,
        hat_in,
        inv_in,
        head_cols,
        prob_soft,
    )
    rewards = lax.dynamic_slice_in_dim(rewards[:, 0], plane_index, 1)
    cell_grads = cell_grads[:, :cell_entries]
    cell_grads = cell_grads.reshape(
        planes, patch_rows, patch_cols, 3, half_patch, half_patch
    ).transpose(0, 3, 1, 4, 2, 5)
    back_image = jnp.pad(
        cell_grads.reshape(planes, 3, rows_total, col_count), ((0, 0), (0, 0), (1, 1), (0, 0))
    )
    slabs_back = jnp.stack(
        [back_image[:, :, r * rows_here : r * rows_here + out_rows] for r in range(row_devices)]
    ).reshape(row_devices * planes, rim_entries, col_count)
    returned = exchange(
        fill(slabs_back, (row_devices * planes, up16(rim_entries), 128)),
        ("rows",) + split_axes + ("tp",),
        tp_devices,
        4,
    )
    returned = returned[:, :rim_entries, :col_count].astype(jnp.float32)
    by_slot = jnp.sum(
        returned.reshape(row_devices, planes * tp_devices, rim_entries * col_count), axis=1
    ).astype(jnp.bfloat16)
    dpicture = jnp.dot(selector.T, by_slot, preferred_element_type=jnp.float32).astype(jnp.bfloat16)
    grad_rimmed = dpicture.reshape(slab_imgs, 3, out_rows, col_count).transpose(1, 0, 2, 3)
    grad_padded = jnp.pad(grad_rimmed, ((0, 0), (0, 0), (0, 0), (1, 1)))
    windows = []
    for offset_y in range(3):
        for offset_x in range(3):
            windows.append(
                grad_padded[
                    :,
                    :,
                    2 - offset_y : 2 - offset_y + rows_here,
                    2 - offset_x : 2 - offset_x + col_count,
                ]
            )
    stacked = jnp.stack(windows, axis=1).reshape(27, -1)
    dactive = lax.dot_general(
        stacked, kernel_rows, (((0,), (0,)), ((), ())), preferred_element_type=jnp.float32
    )
    dactive = dactive.reshape(slab_imgs, rows_here, flat_width)
    gated_grad = dactive * slope_silu * gain_flat
    back_sums = rows_total_sum(
        jnp.stack([channel_group_sums(gated_grad), channel_group_sums(gated_grad * normed)]), 5
    )
    back_one = back_sums[0] / count_group
    back_two = back_sums[1] / count_group
    grad_features = spread_flat(inverse) * (
        gated_grad - spread_flat(back_one) - normed * spread_flat(back_two)
    )
    grad_out = grad_features.astype(jnp.bfloat16).reshape(slab_imgs, rows_here, 1, flat_width)
    return (grad_out, rewards)


def solution(mesh):
    placed = (
        P(("grp", "img"), "rows", "tp", None),
        P("tp"),
        P(None, None, None, "tp"),
        P("rows", None),
        P(),
        P(),
        P("rows", None, "tp"),
        P("rows", "tp"),
        P(),
        P(),
        P(("grp", "img"), None),
    )
    return jax.shard_map(
        body,
        mesh=mesh,
        in_specs=placed,
        out_specs=(P(("grp", "img"), "rows", "tp", None), P(("grp", "img", "rows"))),
        check_vma=False,
    )
```

```python
import functools
import math

import jax
import jax.numpy as jnp
from jax import lax
from jax.experimental import pallas as pl
from jax.experimental.pallas import tpu as pltpu
from jax.sharding import PartitionSpec as P

C = 128
GROUPS = 32
PATCH = 14
HEAD_DIM = 80
W = 112


EPS_GROUP = 1e-06
EPS_LAYER = 1e-05


def exchange_kernel(axes, sizes, pick, x_ref, o_ref, send_sems, recv_sems, local_sem):
    total = math.prod(sizes)
    me = 0
    for axis, size in zip(axes, sizes):
        me = me * size + lax.axis_index(axis)

    def place(offset):
        index = lax.rem(me + offset, total)
        rest = index
        where = {}
        for axis, size in reversed(list(zip(axes, sizes))):
            where[axis] = lax.rem(rest, size)
            rest = rest // size
        return index, where

    def chunk(index):
        return x_ref if pick is None else x_ref.at[index // pick]

    barrier = pltpu.get_barrier_semaphore()
    for offset in range(1, total):
        pl.semaphore_signal(
            barrier, inc=1, device_id=place(offset)[1], device_id_type=pl.DeviceIdType.MESH
        )
    own = pltpu.make_async_copy(chunk(me), o_ref.at[me], local_sem)
    own.start()
    pl.semaphore_wait(barrier, total - 1)
    copies = []
    for offset in range(1, total):
        index, where = place(offset)
        copy = pltpu.make_async_remote_copy(
            src_ref=chunk(index),
            dst_ref=o_ref.at[me],
            send_sem=send_sems.at[offset - 1],
            recv_sem=recv_sems.at[offset - 1],
            device_id=where,
            device_id_type=pl.DeviceIdType.MESH,
        )
        copy.start()
        copies.append(copy)
    own.wait()
    for copy in copies:
        copy.wait()


def exchange(values, axes, pick, ident):
    sizes = tuple(lax.axis_size(axis) for axis in axes)
    total = math.prod(sizes)
    item = values.shape if pick is None else values.shape[1:]
    size_out = total * math.prod(item) * values.dtype.itemsize
    space = pltpu.VMEM if size_out <= 4 * 2**20 else pl.ANY
    return pl.pallas_call(
        functools.partial(exchange_kernel, axes, sizes, pick),
        out_shape=jax.ShapeDtypeStruct((total,) + item, values.dtype),
        in_specs=[pl.BlockSpec(memory_space=space)],
        out_specs=pl.BlockSpec(memory_space=space),
        scratch_shapes=[
            pltpu.SemaphoreType.DMA((total - 1,)),
            pltpu.SemaphoreType.DMA((total - 1,)),
            pltpu.SemaphoreType.DMA,
        ],
        compiler_params=pltpu.CompilerParams(collective_id=ident, has_side_effects=True),
    )(values)


def round_half(values):
    return lax.optimization_barrier(values.astype(jnp.bfloat16)).astype(jnp.float32)


def layer_norm(values, scale_vec):
    average = jnp.mean(values, axis=-1, keepdims=True)
    centred = values - average
    spread = jnp.mean(centred * centred, axis=-1, keepdims=True)
    inverse = lax.rsqrt(spread + EPS_LAYER)
    normed = centred * inverse
    return (normed * scale_vec, normed, inverse)


def layer_norm_back(upstream, normed, inverse, scale_vec):
    scaled = upstream * scale_vec
    mean_one = jnp.mean(scaled, axis=-1, keepdims=True)
    mean_two = jnp.mean(scaled * normed, axis=-1, keepdims=True)
    return inverse * (scaled - mean_one - normed * mean_two)


def silu_parts(values):
    sigmoid = jax.nn.sigmoid(values)
    return (values * sigmoid, sigmoid * (1.0 + values * (1.0 - sigmoid)))


def fill(values, sizes):
    return jnp.pad(values, [(0, size - have) for size, have in zip(sizes, values.shape)])


def up16(count):
    return (count + 15) // 16 * 16


def mm(left, right, left_dim, right_dim):
    return lax.dot_general(
        left, right, (((left_dim,), (right_dim,)), ((), ())), preferred_element_type=jnp.float32
    )


def hold(values):
    return values.astype(jnp.bfloat16)


class Windows:
    def __init__(self, span, heads_mine, cell_entries):
        self.fold = (cell_entries + 127) // 128 * 128
        self.heads = heads_mine
        end = self.fold + 3 * span
        self.wide = (end + span + 127) // 128 * 128
        self.high = (end + 127) // 128 * 128
        self.low = end // 128 * 128
        self.end = end

    def select(self, start, stop, first, blocks):
        row = jnp.arange(start, stop, dtype=jnp.int32)[:, None]
        column = jnp.arange(blocks * 128, dtype=jnp.int32)[None, :]
        lane = column % 128
        hit = (row == first + column // 128 * HEAD_DIM + lane) & (lane < HEAD_DIM)
        return hit.astype(jnp.bfloat16)


def cell_masks(rows_of, patch_cols, half_patch, fold):
    columns = patch_cols * half_patch
    place = lax.broadcasted_iota(jnp.int32, (rows_of, patch_cols, 128), 1) * half_patch
    lane = lax.broadcasted_iota(jnp.int32, (rows_of, patch_cols, 128), 2)
    inside = ((lane >= place) & (lane < place + half_patch)).astype(jnp.float32)
    pixel = lax.broadcasted_iota(jnp.int32, (128, fold), 0)
    offset = lax.broadcasted_iota(jnp.int32, (128, fold), 1) - pixel
    for patch in range(1, patch_cols):
        offset = offset + jnp.where(pixel >= patch * half_patch, half_patch, 0)
    offset = jnp.where(pixel < columns, offset, -1)
    return inside.reshape(rows_of * patch_cols, 128), offset


def over(count, step):
    if count == 1:
        step(0)
    else:

        @pl.loop(0, count)
        def _(index):
            step(index)


def scorer_forward(
    win, planes, tokens, per_chunk, half_patch, patch_cols, pics_ref, w_ref, pick_qkv_ref, pick_out_ref, pos_ref, gain_ref,
    hat_ref, inv_ref, heads_ref, prob_ref, mixed_ref, pooled_ref, att_ref,
):
    heads = win.heads
    rows = per_chunk * tokens
    rows_of = rows // patch_cols
    inside, offset = cell_masks(rows_of, patch_cols, half_patch, win.fold)
    factor = 1.0 / math.sqrt(HEAD_DIM)

    def embed(index):
        at = pl.ds(pl.multiple_of(index * rows, rows), rows)
        cells = jnp.zeros((rows, win.fold), jnp.float32)
        lines = pl.ds(pl.multiple_of(index * rows_of, rows_of), rows_of)
        for line in range(pics_ref.shape[0]):
            spread = jnp.broadcast_to(
                pics_ref[line, lines, :][:, None, :], (rows_of, patch_cols, 128)
            ).reshape(rows, 128)
            cells = cells + mm(
                hold(spread * inside), hold((offset == line * half_patch).astype(jnp.float32)), 1, 0
            )
        embedded = mm(hold(cells), w_ref[:, : win.fold], 1, 1)
        width = embedded.shape[1]
        embedded = embedded.reshape(per_chunk, tokens, width) + pos_ref[...].astype(jnp.float32)[None]
        for inner in range(per_chunk):
            pooled_ref[pl.ds(index * per_chunk + inner, 1), :] = jnp.mean(
                embedded[inner], axis=0, keepdims=True
            )
        embedded = embedded.reshape(rows, width)
        normed_in, hat, inverse = layer_norm(embedded, gain_ref[...])
        hat_ref[at, :] = hat
        inv_ref[at, :] = jnp.broadcast_to(inverse, (rows, 128))
        flat = hold(mm(hold(normed_in), w_ref[:, win.fold : win.high], 1, 0))
        heads_ref[at, :] = hold(mm(flat, pick_qkv_ref[...], 1, 0))

    over(planes // per_chunk, embed)

    def attend(plane):
        at = pl.ds(pl.multiple_of(plane * tokens, tokens), tokens)
        for head in range(heads):
            query = heads_ref[at, head * 128 : head * 128 + 128]
            key = heads_ref[at, (heads + head) * 128 : (heads + head) * 128 + 128]
            value = heads_ref[at, (2 * heads + head) * 128 : (2 * heads + head) * 128 + 128]
            scores = mm(query, key, 1, 1) * factor
            exp_scores = jnp.exp(scores - jnp.max(scores, axis=-1, keepdims=True))
            prob = exp_scores / jnp.sum(exp_scores, axis=-1, keepdims=True)
            prob_ref[at, head * tokens : head * tokens + tokens] = prob
            mean_row = (
                jnp.sum(hold(prob).astype(jnp.float32), axis=0, keepdims=True) * (1.0 / tokens)
            )
            mean_high = hold(mean_row)
            mean_low = hold(mean_row - mean_high.astype(jnp.float32))
            att_ref[pl.ds(plane, 1), head * 128 : head * 128 + 128] = mm(
                mean_high, value, 1, 0
            ) + mm(mean_low, value, 1, 0)

    if planes * heads <= 8 and tokens <= 64:
        for plane in range(planes):
            attend(plane)
    else:
        over(planes, attend)
    attended = att_ref[...]
    high = hold(attended)
    low = hold(attended - high.astype(jnp.float32))
    out_window = w_ref[:, win.low :]
    mixed_ref[...] = mm(hold(mm(high, pick_out_ref[...], 1, 1)), out_window, 1, 1) + mm(
        hold(mm(low, pick_out_ref[...], 1, 1)), out_window, 1, 1
    )


def scorer_backward(
    win, planes, tokens, per_chunk, half_patch, patch_cols, mixed_ref, pooled_ref, final_ref, head_w_ref, first_ref, w_ref,
    pick_qkv_ref, pick_out_ref, gain_ref, hat_ref, inv_ref, heads_ref, prob_ref,
    dpics_ref, reward_ref, grad_ref, up_ref, share_ref,
):
    heads = win.heads
    rows = per_chunk * tokens
    rows_of = rows // patch_cols
    inside, offset = cell_masks(rows_of, patch_cols, half_patch, win.fold)
    factor = 1.0 / math.sqrt(HEAD_DIM)
    pooled = pooled_ref[...]
    for index in range(mixed_ref.shape[0]):
        pooled = pooled + mixed_ref[index]
    final_gain = final_ref[...]
    head_w = head_w_ref[...]
    pooled_out, hat_z, inv_z = layer_norm(pooled, final_gain)
    reward_ref[...] = jnp.broadcast_to(
        jnp.sum(pooled_out * head_w, axis=-1, keepdims=True), reward_ref.shape
    )
    upstream = layer_norm_back(head_w, hat_z, inv_z, final_gain)
    up_ref[...] = upstream * first_ref[0:1, 0:1]
    share_ref[...] = mm(
        hold(mm(hold(upstream), w_ref[:, win.low :], 1, 0)), pick_out_ref[...], 1, 0
    )

    def attend(plane):
        at = pl.ds(pl.multiple_of(plane * tokens, tokens), tokens)
        for head in range(heads):
            lanes = [
                slice((which * heads + head) * 128, (which * heads + head) * 128 + 128)
                for which in range(3)
            ]
            query, key, value = (heads_ref[at, lane] for lane in lanes)
            prob = prob_ref[at, head * tokens : head * tokens + tokens]
            share = hold(
                jnp.broadcast_to(
                    share_ref[pl.ds(plane, 1), head * 128 : head * 128 + 128], (tokens, 128)
                )
            )
            dprob = mm(share, value, 1, 1)
            dscores = hold(
                prob * (dprob - jnp.sum(dprob * prob, axis=-1, keepdims=True)) * factor
            )
            grad_ref[at, lanes[0]] = hold(mm(dscores, key, 1, 0))
            grad_ref[at, lanes[1]] = hold(mm(dscores, query, 0, 0))
            grad_ref[at, lanes[2]] = hold(mm(hold(prob), share, 0, 0))

    if planes * heads <= 8 and tokens <= 64:
        for plane in range(planes):
            attend(plane)
    else:
        over(planes, attend)

    def finish(index):
        at = pl.ds(pl.multiple_of(index * rows, rows), rows)
        flat = hold(mm(grad_ref[at, :], pick_qkv_ref[...], 1, 1))
        dnormed = mm(flat, w_ref[:, win.fold : win.high], 1, 1)
        dlinear = layer_norm_back(dnormed, hat_ref[at, :], inv_ref[at, 0:1], gain_ref[...])
        width = dlinear.shape[1]
        dlinear = dlinear.reshape(per_chunk, tokens, width)
        pieces = [
            dlinear[inner] + up_ref[pl.ds(index * per_chunk + inner, 1), :]
            for inner in range(per_chunk)
        ]
        dembedded = hold(jnp.concatenate(pieces, axis=0) if per_chunk > 1 else pieces[0])
        dcells = hold(mm(dembedded, w_ref[:, : win.fold], 1, 0))
        lines = pl.ds(pl.multiple_of(index * rows_of, rows_of), rows_of)
        for line in range(dpics_ref.shape[0]):
            spread = inside * mm(
                dcells, hold((offset == line * half_patch).astype(jnp.float32)), 1, 1
            )
            dpics_ref[line, lines, :] = jnp.sum(spread.reshape(rows_of, patch_cols, 128), axis=1)

    over(planes // per_chunk, finish)


def local_call(kernel, shapes, scratch, *operands):
    vmem = pl.BlockSpec(memory_space=pltpu.VMEM)
    return pl.pallas_call(
        kernel,
        out_shape=shapes,
        in_specs=[vmem] * len(operands),
        out_specs=[vmem] * len(shapes),
        scratch_shapes=scratch,
        compiler_params=pltpu.CompilerParams(vmem_limit_bytes=56 * 2**20),
    )(*operands)


def body(
    features,
    gn_gain,
    conv_w,
    patch_w,
    pos_emb,
    ln1_gain,
    qkv_w,
    out_w,
    final_gain,
    head_w,
    owner_slot,
):
    slab_imgs, rows_here, _, flat_width = features.shape
    col_count = W
    chan_count = flat_width // col_count
    row_devices = lax.axis_size("rows")
    rows_total = rows_here * row_devices
    groups_here = GROUPS * chan_count // C
    group_width = chan_count // groups_here
    count_group = rows_total * col_count * group_width
    half_patch = PATCH // 2
    patch_rows = rows_total // half_patch
    patch_cols = col_count // half_patch

    tp_devices = lax.axis_size("tp")
    feat_own, _, half_width = qkv_w.shape
    width = pos_emb.shape[1]
    heads_half = half_width // HEAD_DIM
    split_axes = ("grp", "img")
    if heads_half % (lax.axis_size("grp") * lax.axis_size("img")):
        split_axes = ("img",)
    planes = math.prod(lax.axis_size(axis) for axis in split_axes)
    plane_index = 0
    for axis in split_axes:
        plane_index = plane_index * lax.axis_size(axis) + lax.axis_index(axis)
    heads_mine = heads_half // planes
    span = heads_mine * HEAD_DIM
    cell_entries = 3 * half_patch * half_patch
    entry_index = jnp.arange(3 * PATCH * PATCH, dtype=jnp.int32)
    pixel_index = entry_index // 3
    target = (
        entry_index % 3 * half_patch * half_patch
        + pixel_index // PATCH // 2 * half_patch
        + pixel_index % PATCH // 2
    )
    fold_table = (
        target[:, None] == jnp.arange(cell_entries, dtype=jnp.int32)[None, :]
    ).astype(jnp.bfloat16)
    folded_own = jnp.dot(patch_w, fold_table, preferred_element_type=jnp.float32)
    win = Windows(span, heads_mine, cell_entries)
    weights_own = jnp.concatenate(
        [
            fill(folded_own.astype(jnp.bfloat16), (feat_own, win.fold)),
            lax.dynamic_slice_in_dim(qkv_w, plane_index * span, span, 2).reshape(feat_own, 3 * span),
            lax.dynamic_slice_in_dim(out_w, plane_index * span, span, 1),
        ],
        axis=1,
    )
    weights = lax.all_gather(fill(weights_own, (feat_own, win.wide)), "rows", axis=0, tiled=True)
    pick_qkv = win.select(win.fold, win.high, win.fold, 3 * heads_mine)
    pick_out = win.select(win.low, win.wide, win.end, heads_mine)

    def channel_group_sums(flat):
        per_col = jnp.sum(flat, axis=1).reshape(slab_imgs, col_count, chan_count)
        per_chan = jnp.sum(per_col, axis=1)
        return jnp.sum(per_chan.reshape(slab_imgs, groups_here, group_width), axis=2)

    def rows_total_sum(values, ident):
        flat = fill(values.reshape(2 * slab_imgs, groups_here), (2 * slab_imgs, 128))
        summed = jnp.sum(exchange(flat, ("rows",), None, ident), axis=0)
        return summed[:, :groups_here].reshape(2, slab_imgs, groups_here)

    def spread_flat(per_group):
        return jnp.tile(jnp.repeat(per_group, group_width, axis=1), (1, col_count))[:, None, :]

    feat_float = features.reshape(slab_imgs, rows_here, flat_width).astype(jnp.float32)
    stat_sums = rows_total_sum(
        jnp.stack([channel_group_sums(feat_float), channel_group_sums(feat_float * feat_float)]), 1
    )
    average = stat_sums[0] / count_group
    inverse = lax.rsqrt(stat_sums[1] / count_group - average * average + EPS_GROUP)
    gain_flat = jnp.tile(gn_gain, col_count)[None, None, :]
    normed = (feat_float - spread_flat(average)) * spread_flat(inverse)
    scaled = normed * gain_flat
    active, slope_silu = silu_parts(scaled)
    active = active.astype(jnp.bfloat16)
    kernel_rows = conv_w.reshape(27, chan_count)
    widened = jnp.pad(active, ((0, 0), (2, 2), (0, 0)))
    block_rows = widened.shape[1]
    padded = jnp.pad(widened, ((0, 0), (0, 0), (chan_count, chan_count)))
    terms = lax.dot_general(
        kernel_rows,
        padded.reshape(-1, chan_count),
        (((1,), (1,)), ((), ())),
        preferred_element_type=jnp.float32,
    )
    shifted_terms = terms.reshape(3, 3, 3, slab_imgs, block_rows, col_count + 2)
    out_rows = rows_here + 2
    total = jnp.zeros((3, slab_imgs, out_rows, col_count), jnp.float32)
    for shifted_offset_y in range(3):
        for shifted_offset_x in range(3):
            total = (
                total
                + shifted_terms[
                    :,
                    shifted_offset_y,
                    shifted_offset_x,
                    :,
                    shifted_offset_y : shifted_offset_y + out_rows,
                    shifted_offset_x : shifted_offset_x + col_count,
                ]
            )
    mine = lax.axis_index("rows")
    tokens = patch_rows * patch_cols
    rim_entries = 3 * out_rows
    slot_of = owner_slot[0]
    slot_ids = jnp.arange(slab_imgs, dtype=jnp.int32)
    selector = (slot_of[None, :] == slot_ids[:, None]).astype(jnp.bfloat16)
    partial = total.transpose(1, 0, 2, 3).reshape(slab_imgs, -1).astype(jnp.bfloat16)
    ordered = jnp.dot(selector, partial, preferred_element_type=jnp.float32).astype(jnp.bfloat16)
    ordered = ordered.reshape(slab_imgs, rim_entries, col_count)
    slabs = exchange(
        fill(ordered, (slab_imgs, up16(rim_entries), 128)),
        ("rows",) + split_axes + ("tp",),
        planes * tp_devices,
        2,
    )
    slabs = slabs[:, :rim_entries].astype(jnp.float32)
    slabs = slabs.reshape(row_devices, planes, tp_devices, 3, out_rows, 128)
    slabs = jnp.sum(slabs, axis=2)
    middle = slabs[:, :, :, 1:-1]
    above = jnp.pad(slabs[:-1, :, :, -1:], ((1, 0), (0, 0), (0, 0), (0, rows_here - 1), (0, 0)))
    below = jnp.pad(slabs[1:, :, :, :1], ((0, 1), (0, 0), (0, 0), (rows_here - 1, 0), (0, 0)))
    picture = (middle + above + below).astype(jnp.bfloat16).astype(jnp.float32)
    picture_lines = picture.transpose(2, 3, 1, 0, 4).reshape(
        3 * half_patch, planes * patch_rows, 128
    )
    total_rows = planes * tokens
    per_chunk = max(1, min(planes, 256 // tokens))
    shape = jax.ShapeDtypeStruct
    gain_row = ln1_gain[None]
    hat_in, inv_in, head_cols, prob_soft, mixed, pooled_in = local_call(
        functools.partial(
            scorer_forward, win, planes, tokens, per_chunk, half_patch, patch_cols
        ),
        [
            shape((total_rows, width), jnp.float32),
            shape((total_rows, 128), jnp.float32),
            shape((total_rows, 3 * heads_mine * 128), jnp.bfloat16),
            shape((total_rows, heads_mine * tokens), jnp.float32),
            shape((planes, width), jnp.float32),
            shape((planes, width), jnp.float32),
        ],
        [pltpu.VMEM((planes, heads_mine * 128), jnp.float32)],
        picture_lines,
        weights,
        pick_qkv,
        pick_out,
        pos_emb,
        gain_row,
    )
    mixed = exchange(mixed, split_axes + ("tp",), None, 3)
    first = jnp.where(plane_index + lax.axis_index("tp") == 0, 1.0, 0.0)
    cell_grads, rewards = local_call(
        functools.partial(
            scorer_backward, win, planes, tokens, per_chunk, half_patch, patch_cols
        ),
        [
            shape((3 * half_patch, planes * patch_rows, 128), jnp.float32),
            shape((planes, 128), jnp.float32),
        ],
        [
            pltpu.VMEM((total_rows, 3 * heads_mine * 128), jnp.bfloat16),
            pltpu.VMEM((planes, width), jnp.float32),
            pltpu.VMEM((planes, heads_mine * 128), jnp.float32),
        ],
        mixed,
        pooled_in,
        final_gain[None],
        head_w[None],
        jnp.broadcast_to(first, (1, 128)),
        weights,
        pick_qkv,
        pick_out,
        gain_row,
        hat_in,
        inv_in,
        head_cols,
        prob_soft,
    )
    rewards = lax.dynamic_slice_in_dim(rewards[:, 0], plane_index, 1)
    cell_grads = cell_grads.astype(jnp.bfloat16).reshape(3, half_patch, planes, patch_rows, 128)
    back_image = jnp.pad(
        cell_grads.transpose(2, 0, 3, 1, 4).reshape(planes, 3, rows_total, 128),
        ((0, 0), (0, 0), (1, 1), (0, 0)),
    )
    slabs_back = jnp.stack(
        [back_image[:, :, r * rows_here : r * rows_here + out_rows] for r in range(row_devices)]
    ).reshape(row_devices * planes, rim_entries, 128)
    returned = exchange(
        fill(slabs_back, (row_devices * planes, up16(rim_entries), 128)),
        ("rows",) + split_axes + ("tp",),
        tp_devices,
        4,
    )
    returned = returned[:, :rim_entries, :col_count].astype(jnp.float32)
    by_slot = jnp.sum(
        returned.reshape(row_devices, planes * tp_devices, rim_entries * col_count), axis=1
    ).astype(jnp.bfloat16)
    dpicture = jnp.dot(selector.T, by_slot, preferred_element_type=jnp.float32).astype(jnp.bfloat16)
    grad_rimmed = dpicture.reshape(slab_imgs, 3, out_rows, col_count).transpose(1, 0, 2, 3)
    grad_padded = jnp.pad(grad_rimmed, ((0, 0), (0, 0), (0, 0), (1, 1)))
    windows = []
    for offset_y in range(3):
        for offset_x in range(3):
            windows.append(
                grad_padded[
                    :,
                    :,
                    2 - offset_y : 2 - offset_y + rows_here,
                    2 - offset_x : 2 - offset_x + col_count,
                ]
            )
    stacked = jnp.stack(windows, axis=1).reshape(27, -1)
    dactive = lax.dot_general(
        stacked, kernel_rows, (((0,), (0,)), ((), ())), preferred_element_type=jnp.float32
    )
    dactive = dactive.reshape(slab_imgs, rows_here, flat_width)
    gated_grad = dactive * slope_silu * gain_flat
    back_sums = rows_total_sum(
        jnp.stack([channel_group_sums(gated_grad), channel_group_sums(gated_grad * normed)]), 5
    )
    back_one = back_sums[0] / count_group
    back_two = back_sums[1] / count_group
    grad_features = spread_flat(inverse) * (
        gated_grad - spread_flat(back_one) - normed * spread_flat(back_two)
    )
    grad_out = grad_features.astype(jnp.bfloat16).reshape(slab_imgs, rows_here, 1, flat_width)
    return (grad_out, rewards)


def solution(mesh):
    placed = (
        P(("grp", "img"), "rows", "tp", None),
        P("tp"),
        P(None, None, None, "tp"),
        P("rows", None),
        P(),
        P(),
        P("rows", None, "tp"),
        P("rows", "tp"),
        P(),
        P(),
        P(("grp", "img"), None),
    )
    return jax.shard_map(
        body,
        mesh=mesh,
        in_specs=placed,
        out_specs=(P(("grp", "img"), "rows", "tp", None), P(("grp", "img", "rows"))),
        check_vma=False,
    )
```
